256 devices in a mesh: seq: 8 (over z_lo, x), head: 32 (over z_hi, y, core).
Axes of the slice: x: 4, y: 4, z: 8 (z_hi: 4, z_lo: 2; z = z_hi * 2 + z_lo), core: 2. Of those that a mesh axis runs over, the one named last changes fastest.
Arguments:
- queries: bfloat16 [8192, 8192], P('seq', 'head'), may hold values from -8 to 8
- key_cols: bfloat16 [1024, 8192], P('head', 'seq'), may hold values from -8 to 8
- value_cols: bfloat16 [1024, 8192], P('head', 'seq'), may hold values from -6 to 6
- grad_out: bfloat16 [8192, 8192], P('seq', 'head'), may hold values from -6 to 6
- key_blocks: int32 [64, 24], replicated, may hold values from 0 to 63, as said below
- block_count: int32 [64], replicated, may hold values from 1 to 24
Outputs:
- attn_out: bfloat16 [8192, 8192], P('seq', 'head')
- grad_query: bfloat16 [8192, 8192], P('seq', 'head')
- grad_key_cols: bfloat16 [1024, 8192], P('head', 'seq')
- grad_value_cols: bfloat16 [1024, 8192], P('head', 'seq')
The draws below stay inside these ranges and needn't reach their ends.
Inputs may be any that keep to these rules, and one draw needn't show every extreme that they name: `key_blocks`: in row a, the live entries are distinct key blocks not after a, in falling order, the first being a itself; entries after the live ones are ignored.
All inputs are finite; a program needn't handle non-finite values.
Results may differ from the reference program's by a relative error of at most 0.02.
Values may be sent and summed in bfloat16 or wider, within the bound.
No kernel may reach another device: no remote copies, remote signals or barrier semaphores. Data moves between devices by JAX's collectives and lax.ppermute only.
A program may use at most 128 MiB of HBM per device.

```python
import math
import jax
import jax.numpy as jnp
from jax import lax

DH = 128
GROUP = 8
BLK = 128
NNZ = 24
BAND = 8
STRIDE = 3
HQ = 64
KVH = 8
SEQ = 8192
NQB = 64


def draw_key_cols(key, part):
    values = jnp.clip(jax.random.normal(jax.random.fold_in(key, 1), (KVH * DH, SEQ), jnp.float32), -6.0, 6.0)
    return values.astype(jnp.bfloat16)


def draw_queries(key, part):
    values = jnp.clip(jax.random.normal(jax.random.fold_in(key, 2), (SEQ, HQ, DH), jnp.float32), -6.0, 6.0)
    return values.reshape(SEQ, HQ * DH).astype(jnp.bfloat16)


def pattern_tables(key):
    tile_rows = jnp.arange(NQB, dtype=jnp.int32)[:, None]
    slot_ids = jnp.arange(NNZ, dtype=jnp.int32)[None, :]
    offsets = jax.random.randint(jax.random.fold_in(key, 21), (NQB, NNZ), 0, STRIDE)
    offsets = jnp.where(tile_rows == NQB - 1, 0, offsets)
    band_keys = tile_rows - slot_ids
    far_keys = tile_rows - BAND - (slot_ids - BAND) * STRIDE - offsets
    tile_keys = jnp.where(slot_ids < BAND, band_keys, far_keys)
    is_valid = tile_keys >= 0
    extra_slots = jax.random.randint(jax.random.fold_in(key, 22), (NQB, 1), 0, NNZ - BAND + 1)
    band_cut = jax.random.randint(jax.random.fold_in(key, 23), (NQB, 1), 1, BAND + 1)
    slot_limit = jnp.where(tile_rows < BAND, band_cut, BAND + extra_slots)
    slot_limit = jnp.where(tile_rows == NQB - 1, NNZ, slot_limit)
    live_slots = is_valid & (slot_ids < slot_limit)
    live_count = jnp.sum(live_slots.astype(jnp.int32), axis=1)
    filler = jax.random.randint(jax.random.fold_in(key, 24), (NQB, NNZ), 0, NQB)
    filler = filler % (tile_rows + 1)
    chosen = jnp.where(live_slots, tile_keys, filler)
    return (chosen.astype(jnp.int32), live_count.astype(jnp.int32))


def draw_key_blocks(key, part):
    return pattern_tables(jax.random.fold_in(key, 31))[0]


def draw_block_count(key, part):
    return pattern_tables(jax.random.fold_in(key, 31))[1]


def block_levels(stream_key, extent, split, least, largest):
    gain = 1.0
    for axis_at, shards_of in split:
        heights = jax.random.uniform(jax.random.fold_in(jax.random.fold_in(stream_key, 6), axis_at), (shards_of,), jnp.float32, least / len(split), largest / len(split))
        gain = gain * jnp.repeat(jnp.exp(heights), extent[axis_at] // shards_of).reshape((-1,) + (1,) * (len(extent) - 1 - axis_at))
    return gain


def scatter_about(stream_key, shape, scale, limit, shards=(), held_as=jnp.bfloat16):
    factor_of = block_levels(stream_key, shape, shards, -0.22, 0.18) if shards else 1.0
    values = jax.random.normal(stream_key, shape, jnp.float32) * scale * factor_of
    return jnp.minimum(jnp.maximum(values, -limit), limit).astype(held_as)


def setup_inputs(seed: int = 0) -> dict:
    arg_keys = jax.random.split(jax.random.key(seed), 7)
    queries = draw_queries(jax.random.fold_in(arg_keys[6], 71), 0)
    key_cols = draw_key_cols(jax.random.fold_in(arg_keys[6], 71), 0)
    value_cols = scatter_about(arg_keys[2], (KVH * DH, SEQ), 1.0, 6.0, ((0, 32), (1, 8)))
    grad_out = scatter_about(arg_keys[3], (SEQ, HQ * DH), 1.0, 6.0, ((0, 8), (1, 32)))
    key_blocks = draw_key_blocks(jax.random.fold_in(arg_keys[6], 71), 0)
    block_count = draw_block_count(jax.random.fold_in(arg_keys[6], 71), 0)
    return dict(queries=queries, key_cols=key_cols, value_cols=value_cols, grad_out=grad_out, key_blocks=key_blocks, block_count=block_count)


def block_pass(query_block, out_grad, key_tiles, value_tiles, tile_ids, tile_count, query_tile):
    block_rows = query_block.shape[0]
    head_dims = query_block.shape[2]
    slot_total = tile_ids.shape[0]
    scaling = 1.0 / math.sqrt(head_dims)
    key_pick = jnp.take(key_tiles, tile_ids, axis=1).astype(jnp.float32)
    value_pick = jnp.take(value_tiles, tile_ids, axis=1).astype(jnp.float32)
    query_wide = query_block.astype(jnp.float32)
    grad_wide = out_grad.astype(jnp.float32)
    scores = jnp.einsum('thd,dnk->htnk', query_wide, key_pick) * scaling
    query_pos = query_tile * block_rows + jnp.arange(block_rows, dtype=jnp.int32)
    key_pos = tile_ids[:, None] * block_rows + jnp.arange(block_rows, dtype=jnp.int32)[None, :]
    live_slot = jnp.arange(slot_total, dtype=jnp.int32) < tile_count
    allowed = live_slot[None, :, None] & (key_pos[None, :, :] <= query_pos[:, None, None])
    masked = jnp.where(allowed[None], scores, -1e+30)
    row_top = lax.optimization_barrier(jnp.max(masked, axis=(2, 3), keepdims=True))
    row_total = lax.optimization_barrier(jnp.sum(jnp.where(allowed[None], jnp.exp(masked - row_top), 0.0), axis=(2, 3), keepdims=True))
    log_total = row_top + jnp.log(row_total)
    weights = jnp.where(allowed[None], jnp.exp(masked - log_total), 0.0)
    weights_low = weights.astype(jnp.bfloat16)
    low_wide = weights_low.astype(jnp.float32)
    attended = jnp.einsum('htnk,dnk->thd', low_wide, value_pick).astype(jnp.bfloat16)
    row_dot = lax.optimization_barrier(jnp.sum(grad_wide * attended.astype(jnp.float32), axis=2))
    grad_weights = jnp.einsum('thd,dnk->htnk', grad_wide, value_pick)
    grad_scores = (weights * (grad_weights - jnp.transpose(row_dot)[:, :, None, None]) * scaling).astype(jnp.bfloat16)
    scores_wide = grad_scores.astype(jnp.float32)
    grad_query = jnp.einsum('htnk,dnk->thd', scores_wide, key_pick).astype(jnp.bfloat16)
    grad_keys = jnp.einsum('htnk,thd->dnk', scores_wide, query_wide)
    grad_values = jnp.einsum('htnk,thd->dnk', low_wide, grad_wide)
    return (attended, grad_query, grad_keys, grad_values)

def reference(queries, key_cols, value_cols, grad_out, key_blocks, block_count):
    seq_len = queries.shape[0]
    tile_total = seq_len // BLK
    kv_heads = key_cols.shape[0] // DH
    query_grid = queries.reshape(tile_total, BLK, kv_heads, GROUP, DH)
    grad_grid = grad_out.reshape(tile_total, BLK, kv_heads, GROUP, DH)
    key_grid = key_cols.reshape(kv_heads, DH, tile_total, BLK)
    value_grid = value_cols.reshape(kv_heads, DH, tile_total, BLK)

    def one_head(head_id):
        query_head = lax.dynamic_index_in_dim(query_grid, head_id, 2, keepdims=False)
        grad_head = lax.dynamic_index_in_dim(grad_grid, head_id, 2, keepdims=False)
        key_tiles = lax.dynamic_index_in_dim(key_grid, head_id, 0, keepdims=False)
        value_tiles = lax.dynamic_index_in_dim(value_grid, head_id, 0, keepdims=False)

        def advance(running, inputs):
            key_sums, value_sums = running
            query_block, out_grad, tile_ids, tile_count, query_tile = inputs
            attended, grad_query, grad_keys, grad_values = block_pass(query_block, out_grad, key_tiles, value_tiles, tile_ids, tile_count, query_tile)
            key_sums = key_sums.at[:, tile_ids, :].add(grad_keys)
            value_sums = value_sums.at[:, tile_ids, :].add(grad_values)
            return ((key_sums, value_sums), (attended, grad_query))
        zeros_sum = jnp.zeros((DH, tile_total, BLK), jnp.float32)
        tile_index = jnp.arange(tile_total, dtype=jnp.int32)
        (key_sums, value_sums), (attended, grad_query) = lax.scan(advance, (zeros_sum, zeros_sum), (query_head, grad_head, key_blocks, block_count, tile_index))
        return (attended, grad_query, key_sums.astype(jnp.bfloat16), value_sums.astype(jnp.bfloat16))
    attended, grad_query, key_grads, value_grads = lax.map(one_head, jnp.arange(kv_heads, dtype=jnp.int32))
    attn_out = jnp.transpose(attended, (1, 2, 0, 3, 4)).reshape(seq_len, kv_heads * GROUP * DH)
    grad_q_out = jnp.transpose(grad_query, (1, 2, 0, 3, 4)).reshape(seq_len, kv_heads * GROUP * DH)
    grad_key_cols = key_grads.reshape(kv_heads * DH, seq_len)
    grad_value_cols = value_grads.reshape(kv_heads * DH, seq_len)
    return (attn_out, grad_q_out, grad_key_cols, grad_value_cols)
```

```python
import math

import jax
import jax.numpy as jnp
from jax import lax
from jax.experimental import pallas as pl
from jax.experimental.pallas import tpu as pltpu
from jax.sharding import PartitionSpec as P

DH = 128
HQ_DEV = 2
BLK = 128
GRP = 4
QUARTER = 32
NEG = -1e30
SCALE = 1.0 / math.sqrt(DH)
LOG2E = 1.4426950408889634
NT = (((1,), (1,)), ((), ()))


def dot(left, right):
    return jnp.dot(left, right, preferred_element_type=jnp.float32)


def dot_nt(left, right):
    return lax.dot_general(left, right, NT, preferred_element_type=jnp.float32)


def attend_kernel(
    where_ref, blocks_ref, count_ref,
    q_ref, do_ref, ka_ref, kc_ref, va_ref, vb_ref, vc_ref, vd_ref,
    o_ref, dq_ref, k_keep, k_send, v_keep, v_send,
    kbuf, vbuf, dk, dv, scores, stage, in_sem, out_sem,
):
    seq = where_ref[0]
    quarter = where_ref[1]

    def rows_of(index):
        return pl.ds(pl.multiple_of(index * QUARTER, QUARTER), QUARTER)

    mine, other_y = rows_of(quarter), rows_of(quarter ^ 2)
    sib, sib_y = rows_of(quarter ^ 1), rows_of(quarter ^ 3)
    loads = []
    for src, dst in (
        (ka_ref.at[:, 0], kbuf.at[:, mine]),
        (ka_ref.at[:, 1], kbuf.at[:, other_y]),
        (kc_ref.at[:, 0], kbuf.at[:, sib]),
        (kc_ref.at[:, 1], kbuf.at[:, sib_y]),
        (va_ref, vbuf.at[:, mine]),
        (vb_ref, vbuf.at[:, other_y]),
        (vc_ref, vbuf.at[:, sib]),
        (vd_ref, vbuf.at[:, sib_y]),
    ):
        loads.append(pltpu.make_async_copy(src, dst, in_sem.at[len(loads)]))
    for load in loads:
        load.start()
    for shard in range(8):
        dk[shard] = jnp.zeros((DH, 1024), jnp.float32)
        dv[shard] = jnp.zeros((DH, 1024), jnp.float32)
    for load in loads:
        load.wait()

    def place(block):
        return block // 8, pl.ds(pl.multiple_of((block % 8) * BLK, BLK), BLK)

    def pick(buf, ids):
        parts = []
        for block in ids:
            shard, cols = place(block)
            parts.append(buf[shard, :, cols])
        return jnp.concatenate(parts, axis=1)

    def spread(buf, ids, total):
        for k, block in enumerate(ids):
            shard, cols = place(block)
            buf[shard, :, cols] += total[:, k * BLK : (k + 1) * BLK]

    def one_tile(i, carry):
        tile = seq * 8 + i
        live = count_ref[tile]
        rest = live - 1
        tail = rest % GRP
        full = rest // GRP
        rows = pl.ds(pl.multiple_of(i * BLK, BLK), BLK)
        q2 = q_ref[rows, :]
        do2 = do_ref[rows, :]
        q = jnp.concatenate([q2[:, :DH], q2[:, DH:]], axis=0)
        do = jnp.concatenate([do2[:, :DH], do2[:, DH:]], axis=0)

        def first_ids():
            return [tile] + [
                jnp.where(k <= tail, blocks_ref[tile, k], tile) for k in range(1, GRP)
            ]

        def later_ids(g):
            start = 1 + tail + GRP * (g - 1)
            return [blocks_ref[tile, start + k] for k in range(GRP)]

        ids0 = first_ids()
        s = dot(q, pick(kbuf, ids0))
        row = lax.broadcasted_iota(jnp.int32, (2 * BLK, BLK), 0) % BLK
        col = lax.broadcasted_iota(jnp.int32, (2 * BLK, BLK), 1)
        parts = [jnp.where(col <= row, s[:, :BLK], NEG)]
        for k in range(1, GRP):
            parts.append(jnp.where(k <= tail, s[:, k * BLK : (k + 1) * BLK], NEG))
        top = parts[0]
        for part in parts[1:]:
            top = jnp.maximum(top, part)
        scores[0] = jnp.concatenate(parts, axis=1)

        def fold_max(top, s):
            for k in range(GRP):
                top = jnp.maximum(top, s[:, k * BLK : (k + 1) * BLK])
            return top

        def pass_scores(g, top):
            s = dot(q, pick(kbuf, later_ids(g)))
            scores[g] = s
            return fold_max(top, s)

        top = lax.fori_loop(1, full + 1, pass_scores, top)
        peak = jnp.max(top, axis=1, keepdims=True) * (SCALE * LOG2E)

        def forward(g, ids, carry):
            total, out = carry
            p = jnp.exp2(scores[g] * (SCALE * LOG2E) - peak)
            for k in range(GRP):
                total = total + p[:, k * BLK : (k + 1) * BLK]
            out = out + dot_nt(p.astype(jnp.bfloat16), pick(vbuf, ids))
            return total, out

        zero = jnp.zeros((2 * BLK, BLK), jnp.float32)
        carry2 = forward(0, ids0, (zero, zero))
        total, out = lax.fori_loop(1, full + 1, lambda g, c: forward(g, later_ids(g), c), carry2)
        row_total = jnp.sum(total, axis=1, keepdims=True)
        attended = (out * (1.0 / row_total)).astype(jnp.bfloat16)
        o_ref[rows, :] = jnp.concatenate([attended[:BLK], attended[BLK:]], axis=1)
        log_total = peak + jnp.log2(row_total)
        row_dot = jnp.sum(
            do.astype(jnp.float32) * attended.astype(jnp.float32), axis=1, keepdims=True
        )
        q_t = jnp.transpose(q)
        do_t = jnp.transpose(do)

        def backward(g, ids, grad_q):
            w = jnp.exp2(scores[g] * (SCALE * LOG2E) - log_total)
            grad_w = dot(do, pick(vbuf, ids))
            grad_s = (w * (grad_w - row_dot)).astype(jnp.bfloat16)
            spread(dv, ids, dot(do_t, w.astype(jnp.bfloat16)))
            spread(dk, ids, dot(q_t, grad_s))
            return grad_q + dot_nt(grad_s, pick(kbuf, ids))

        grad_q = backward(0, ids0, zero)
        grad_q = lax.fori_loop(1, full + 1, lambda g, c: backward(g, later_ids(g), c), grad_q)
        grad_q = (grad_q * SCALE).astype(jnp.bfloat16)
        dq_ref[rows, :] = jnp.concatenate([grad_q[:BLK], grad_q[BLK:]], axis=1)
        return carry

    lax.fori_loop(0, 8, one_tile, 0)

    stores = []
    for shard in range(8):
        for buf, low, keep, send, scale in (
            (dk, stage.at[0], k_keep, k_send, SCALE),
            (dv, stage.at[1], v_keep, v_send, None),
        ):
            value = buf[shard]
            if scale is not None:
                value = value * scale
            low[shard] = value.astype(jnp.bfloat16)
            for rows, dst in (
                (mine, keep.at[shard, 0]),
                (other_y, keep.at[shard, 1]),
                (sib, send.at[shard, 0]),
                (sib_y, send.at[shard, 1]),
            ):
                copy = pltpu.make_async_copy(low.at[shard, rows], dst, out_sem.at[len(stores)])
                copy.start()
                stores.append(copy)
    for copy in stores:
        copy.wait()


def attend(where, key_blocks, block_count, queries, grad_out, parts):
    whole = pl.BlockSpec(memory_space=pltpu.VMEM)
    scalar = pl.BlockSpec(memory_space=pltpu.SMEM)
    away = pl.BlockSpec(memory_space=pl.ANY)
    half = jax.ShapeDtypeStruct((8, 2, QUARTER, 1024), jnp.bfloat16)
    grid_q = jax.ShapeDtypeStruct(queries.shape, jnp.bfloat16)
    return pl.pallas_call(
        attend_kernel,
        in_specs=[scalar] * 3 + [whole] * 2 + [away] * 6,
        out_specs=[whole] * 2 + [away] * 4,
        out_shape=[grid_q, grid_q, half, half, half, half],
        scratch_shapes=[
            pltpu.VMEM((8, DH, 1024), jnp.bfloat16),
            pltpu.VMEM((8, DH, 1024), jnp.bfloat16),
            pltpu.VMEM((8, DH, 1024), jnp.float32),
            pltpu.VMEM((8, DH, 1024), jnp.float32),
            pltpu.VMEM((6, 2 * BLK, GRP * BLK), jnp.float32),
            pltpu.VMEM((2, 8, DH, 1024), jnp.bfloat16),
            pltpu.SemaphoreType.DMA((8,)),
            pltpu.SemaphoreType.DMA((64,)),
        ],
        compiler_params=pltpu.CompilerParams(vmem_limit_bytes=48 << 20),
        name="attend",
    )(where, key_blocks, block_count, queries, grad_out, *parts)


def swap(value, bit):
    return lax.ppermute(value, "head", [(i, i ^ bit) for i in range(lax.axis_size("head"))])


def send_all(value):
    shards = lax.axis_size("seq")
    return lax.all_to_all(jnp.broadcast_to(value[None], (shards,) + value.shape), "seq", 0, 0)


def per_device(queries, key_cols, value_cols, grad_out, key_blocks, block_count):
    seq_index = lax.axis_index("seq")
    quarter = lax.axis_index("head") & 3
    upper = quarter >> 1 == 1

    v_mine = send_all(value_cols)
    k_pair = jnp.stack([key_cols, swap(key_cols, 2)])
    k_mine = send_all(k_pair)
    v_pair = swap(v_mine, 2)
    v_sib = swap(v_mine, 1)
    v_sib_pair = swap(v_pair, 1)
    k_sib = swap(k_mine, 1)

    where = jnp.stack([seq_index, quarter]).astype(jnp.int32)
    attn_out, grad_query, k_keep, k_send, v_keep, v_send = attend(
        where, key_blocks, block_count, queries, grad_out,
        (k_mine, k_sib, v_mine, v_pair, v_sib, v_sib_pair),
    )

    def add(left, right):
        return left.astype(jnp.float32) + right.astype(jnp.float32)

    v_half = add(v_keep, swap(v_send, 1)).astype(jnp.bfloat16)
    k_half = add(k_keep, swap(k_send, 1)).astype(jnp.bfloat16)
    v_quarter = add(v_half[:, 0], swap(v_half[:, 1], 2)).astype(jnp.bfloat16)
    k_got = lax.all_to_all(k_half, "seq", 0, 0)
    k_sum = jnp.sum(k_got.astype(jnp.float32), axis=0)
    v_got = lax.all_to_all(v_quarter, "seq", 0, 0)
    grad_value = jnp.sum(v_got.astype(jnp.float32), axis=0).astype(jnp.bfloat16)
    grad_key = (k_sum[0] + swap(k_sum[1], 2)).astype(jnp.bfloat16)
    return attn_out, grad_query, grad_key, grad_value


def solution(mesh):
    placed = (P("seq", "head"), P("head", "seq"), P("head", "seq"), P("seq", "head"), P(), P())
    return jax.shard_map(
        per_device,
        mesh=mesh,
        in_specs=placed,
        out_specs=(P("seq", "head"), P("seq", "head"), P("head", "seq"), P("head", "seq")),
        check_vma=False,
    )
```

```python
import math

import jax
import jax.numpy as jnp
from jax import lax
from jax.experimental import pallas as pl
from jax.experimental.pallas import tpu as pltpu
from jax.sharding import PartitionSpec as P

DH = 128
HQ_DEV = 2
BLK = 128
GRP = 4
NNZ = 24
QUARTER = 32
NEG = -1e30
SCALE = 1.0 / math.sqrt(DH)
LOG2E = 1.4426950408889634
NT = (((1,), (1,)), ((), ()))


def dot(left, right):
    return jnp.dot(left, right, preferred_element_type=jnp.float32)


def dot_nt(left, right):
    return lax.dot_general(left, right, NT, preferred_element_type=jnp.float32)


def wide(column):
    return jnp.broadcast_to(column, (column.shape[0], BLK))


def across(tile):
    return jnp.concatenate([tile] * GRP, axis=1)


def attend_kernel(
    where_ref, blocks_ref, count_ref,
    q_ref, do_ref, ka_ref, kc_ref, va_ref, vb_ref, vc_ref, vd_ref,
    o_ref, dq_ref, k_keep, k_send, v_keep, v_send,
    kbuf, vbuf, dk, dv, scores, stage, in_sem, out_sem,
):
    seq = where_ref[0]
    quarter = where_ref[1]

    def rows_of(index):
        return pl.ds(pl.multiple_of(index * QUARTER, QUARTER), QUARTER)

    mine, other_y = rows_of(quarter), rows_of(quarter ^ 2)
    sib, sib_y = rows_of(quarter ^ 1), rows_of(quarter ^ 3)
    loads = []
    for src, dst in (
        (ka_ref.at[:, 0], kbuf.at[:, mine]),
        (ka_ref.at[:, 1], kbuf.at[:, other_y]),
        (kc_ref.at[:, 0], kbuf.at[:, sib]),
        (kc_ref.at[:, 1], kbuf.at[:, sib_y]),
        (va_ref, vbuf.at[:, mine]),
        (vb_ref, vbuf.at[:, other_y]),
        (vc_ref, vbuf.at[:, sib]),
        (vd_ref, vbuf.at[:, sib_y]),
    ):
        loads.append(pltpu.make_async_copy(src, dst, in_sem.at[len(loads)]))
    for load in loads:
        load.start()
    for shard in range(8):
        dk[shard] = jnp.zeros((DH, 1024), jnp.float32)
        dv[shard] = jnp.zeros((DH, 1024), jnp.float32)
    for load in loads:
        load.wait()

    def place(block):
        return block // 8, pl.ds(pl.multiple_of((block % 8) * BLK, BLK), BLK)

    def pick(buf, ids):
        parts = []
        for block in ids:
            shard, cols = place(block)
            parts.append(buf[shard, :, cols])
        return jnp.concatenate(parts, axis=1)

    def spread(buf, ids, total):
        for k, block in enumerate(ids):
            shard, cols = place(block)
            buf[shard, :, cols] += total[:, k * BLK : (k + 1) * BLK]

    def one_tile(i, later):
        tile = seq * 8 + i
        tail = (count_ref[tile] - 1) % GRP
        rows = pl.ds(pl.multiple_of(i * BLK, BLK), BLK)
        q2 = q_ref[rows, :]
        do2 = do_ref[rows, :]
        q = jnp.concatenate([q2[:, :DH], q2[:, DH:]], axis=0)
        do = jnp.concatenate([do2[:, :DH], do2[:, DH:]], axis=0)

        def first_ids():
            return [tile] + [
                jnp.where(k <= tail, blocks_ref[tile, k], tile) for k in range(1, GRP)
            ]

        def later_ids(g):
            start = 1 + tail + GRP * (g - 1)
            return [blocks_ref[tile, start + k] for k in range(GRP)]

        ids0 = first_ids()
        s = dot(q, pick(kbuf, ids0))
        row = lax.broadcasted_iota(jnp.int32, (2 * BLK, BLK), 0) % BLK
        col = lax.broadcasted_iota(jnp.int32, (2 * BLK, BLK), 1)
        parts = [jnp.where(col <= row, s[:, :BLK], NEG)]
        for k in range(1, GRP):
            parts.append(jnp.where(k <= tail, s[:, k * BLK : (k + 1) * BLK], NEG))
        top = parts[0]
        for part in parts[1:]:
            top = jnp.maximum(top, part)
        scores[0] = jnp.concatenate(parts, axis=1)

        def fold_max(top, s):
            for k in range(GRP):
                top = jnp.maximum(top, s[:, k * BLK : (k + 1) * BLK])
            return top

        def pass_scores(g, top):
            s = dot(q, pick(kbuf, later_ids(g)))
            scores[g] = s
            return fold_max(top, s)
        for g in range(1, later + 1):
            top = pass_scores(g, top)
        peak = wide(jnp.max(top, axis=1, keepdims=True) * (SCALE * LOG2E))

        def forward(g, ids, carry):
            p = jnp.exp2(scores[g] * (SCALE * LOG2E) - across(peak))
            values = jnp.concatenate(
                [pick(vbuf, ids), jnp.ones((DH, GRP * BLK), jnp.bfloat16)], axis=0
            )
            return carry + dot_nt(p.astype(jnp.bfloat16), values)

        zero = jnp.zeros((2 * BLK, BLK), jnp.float32)
        both = forward(0, ids0, jnp.zeros((2 * BLK, 2 * DH), jnp.float32))
        for g in range(1, later + 1):
            both = forward(g, later_ids(g), both)
        out, row_total = both[:, :DH], both[:, DH:]
        attended = (out * (1.0 / row_total)).astype(jnp.bfloat16)
        o_ref[rows, :] = jnp.concatenate([attended[:BLK], attended[BLK:]], axis=1)
        log_total = peak + jnp.log2(row_total)
        row_dot = jnp.sum(
            do.astype(jnp.float32) * attended.astype(jnp.float32), axis=1, keepdims=True
        )
        row_dot = across(wide(row_dot))
        log_total = across(log_total)
        q_t = jnp.transpose(q)
        do_t = jnp.transpose(do)

        def backward(g, ids, grad_q):
            w = jnp.exp2(scores[g] * (SCALE * LOG2E) - log_total)
            grad_w = dot(do, pick(vbuf, ids))
            grad_s = (w * (grad_w - row_dot)).astype(jnp.bfloat16)
            spread(dv, ids, dot(do_t, w.astype(jnp.bfloat16)))
            spread(dk, ids, dot(q_t, grad_s))
            return grad_q + dot_nt(grad_s, pick(kbuf, ids))

        grad_q = backward(0, ids0, zero)
        for g in range(1, later + 1):
            grad_q = backward(g, later_ids(g), grad_q)
        grad_q = (grad_q * SCALE).astype(jnp.bfloat16)
        dq_ref[rows, :] = jnp.concatenate([grad_q[:BLK], grad_q[BLK:]], axis=1)

    def any_tile(i, carry):
        full = (count_ref[seq * 8 + i] - 1) // GRP
        for v in range(NNZ // GRP):
            pl.when(full == v)(lambda v=v: one_tile(i, v))
        return carry

    lax.fori_loop(0, 8, any_tile, 0)

    stores = []
    for shard in range(8):
        for buf, low, keep, send, scale in (
            (dk, stage.at[0], k_keep, k_send, SCALE),
            (dv, stage.at[1], v_keep, v_send, None),
        ):
            value = buf[shard]
            if scale is not None:
                value = value * scale
            low[shard] = value.astype(jnp.bfloat16)
            for rows, dst in (
                (mine, keep.at[shard, 0]),
                (other_y, keep.at[shard, 1]),
                (sib, send.at[shard, 0]),
                (sib_y, send.at[shard, 1]),
            ):
                copy = pltpu.make_async_copy(low.at[shard, rows], dst, out_sem.at[len(stores)])
                copy.start()
                stores.append(copy)
    for copy in stores:
        copy.wait()


def attend(where, key_blocks, block_count, queries, grad_out, parts):
    whole = pl.BlockSpec(memory_space=pltpu.VMEM)
    scalar = pl.BlockSpec(memory_space=pltpu.SMEM)
    away = pl.BlockSpec(memory_space=pl.ANY)
    half = jax.ShapeDtypeStruct((8, 2, QUARTER, 1024), jnp.bfloat16)
    grid_q = jax.ShapeDtypeStruct(queries.shape, jnp.bfloat16)
    return pl.pallas_call(
        attend_kernel,
        in_specs=[scalar] * 3 + [whole] * 2 + [away] * 6,
        out_specs=[whole] * 2 + [away] * 4,
        out_shape=[grid_q, grid_q, half, half, half, half],
        scratch_shapes=[
            pltpu.VMEM((8, DH, 1024), jnp.bfloat16),
            pltpu.VMEM((8, DH, 1024), jnp.bfloat16),
            pltpu.VMEM((8, DH, 1024), jnp.float32),
            pltpu.VMEM((8, DH, 1024), jnp.float32),
            pltpu.VMEM((NNZ // GRP, 2 * BLK, GRP * BLK), jnp.float32),
            pltpu.VMEM((2, 8, DH, 1024), jnp.bfloat16),
            pltpu.SemaphoreType.DMA((8,)),
            pltpu.SemaphoreType.DMA((64,)),
        ],
        compiler_params=pltpu.CompilerParams(vmem_limit_bytes=48 << 20),
        name="attend",
    )(where, key_blocks, block_count, queries, grad_out, *parts)


def swap(value, bit):
    return lax.ppermute(value, "head", [(i, i ^ bit) for i in range(lax.axis_size("head"))])


def send_all(value):
    shards = lax.axis_size("seq")
    return lax.all_to_all(jnp.broadcast_to(value[None], (shards,) + value.shape), "seq", 0, 0)


def per_device(queries, key_cols, value_cols, grad_out, key_blocks, block_count):
    seq_index = lax.axis_index("seq")
    quarter = lax.axis_index("head") & 3
    upper = quarter >> 1 == 1

    v_mine = send_all(value_cols)
    k_pair = jnp.stack([key_cols, swap(key_cols, 2)])
    k_mine = send_all(k_pair)
    v_pair = swap(v_mine, 2)
    v_sib = swap(v_mine, 1)
    v_sib_pair = swap(v_pair, 1)
    k_sib = swap(k_mine, 1)

    where = jnp.stack([seq_index, quarter]).astype(jnp.int32)
    attn_out, grad_query, k_keep, k_send, v_keep, v_send = attend(
        where, key_blocks, block_count, queries, grad_out,
        (k_mine, k_sib, v_mine, v_pair, v_sib, v_sib_pair),
    )

    def add(left, right):
        return left.astype(jnp.float32) + right.astype(jnp.float32)

    v_half = add(v_keep, swap(v_send, 1)).astype(jnp.bfloat16)
    k_half = add(k_keep, swap(k_send, 1)).astype(jnp.bfloat16)
    v_quarter = add(v_half[:, 0], swap(v_half[:, 1], 2)).astype(jnp.bfloat16)
    k_got = lax.all_to_all(k_half, "seq", 0, 0)
    k_sum = jnp.sum(k_got.astype(jnp.float32), axis=0)
    v_got = lax.all_to_all(v_quarter, "seq", 0, 0)
    grad_value = jnp.sum(v_got.astype(jnp.float32), axis=0).astype(jnp.bfloat16)
    grad_key = (k_sum[0] + swap(k_sum[1], 2)).astype(jnp.bfloat16)
    return attn_out, grad_query, grad_key, grad_value


def solution(mesh):
    placed = (P("seq", "head"), P("head", "seq"), P("head", "seq"), P("seq", "head"), P(), P())
    return jax.shard_map(
        per_device,
        mesh=mesh,
        in_specs=placed,
        out_specs=(P("seq", "head"), P("seq", "head"), P("head", "seq"), P("head", "seq")),
        check_vma=False,
    )
```

```python
import math

import jax
import jax.numpy as jnp
from jax import lax
from jax.experimental import pallas as pl
from jax.experimental.pallas import tpu as pltpu
from jax.sharding import PartitionSpec as P

DH = 128
HQ_DEV = 2
BLK = 128
GRP = 4
NNZ = 24
QUARTER = 32
NEG = -1e30
SCALE = 1.0 / math.sqrt(DH)
LOG2E = 1.4426950408889634
NT = (((1,), (1,)), ((), ()))


def dot(left, right):
    return jnp.dot(left, right, preferred_element_type=jnp.float32)


def dot_nt(left, right):
    return lax.dot_general(left, right, NT, preferred_element_type=jnp.float32)


def wide(column):
    return jnp.broadcast_to(column, (column.shape[0], BLK))


def across(tile):
    return jnp.concatenate([tile] * GRP, axis=1)


def attend_kernel(
    where_ref, blocks_ref, count_ref,
    q_ref, do_ref, ka_ref, kc_ref, va_ref, vb_ref, vc_ref, vd_ref,
    o_ref, dq_ref, k_keep, k_send, v_keep, v_send,
    kbuf, vbuf, dk, dv, scores, grads, stage, in_sem, out_sem,
):
    seq = where_ref[0]
    quarter = where_ref[1]

    def rows_of(index):
        return pl.ds(pl.multiple_of(index * QUARTER, QUARTER), QUARTER)

    mine, other_y = rows_of(quarter), rows_of(quarter ^ 2)
    sib, sib_y = rows_of(quarter ^ 1), rows_of(quarter ^ 3)
    loads = []
    for src, dst in (
        (ka_ref.at[:, 0], kbuf.at[:, mine]),
        (ka_ref.at[:, 1], kbuf.at[:, other_y]),
        (kc_ref.at[:, 0], kbuf.at[:, sib]),
        (kc_ref.at[:, 1], kbuf.at[:, sib_y]),
        (va_ref, vbuf.at[:, mine]),
        (vb_ref, vbuf.at[:, other_y]),
        (vc_ref, vbuf.at[:, sib]),
        (vd_ref, vbuf.at[:, sib_y]),
    ):
        loads.append(pltpu.make_async_copy(src, dst, in_sem.at[len(loads)]))
    for load in loads:
        load.start()
    for shard in range(8):
        dk[shard] = jnp.zeros((DH, 1024), jnp.float32)
        dv[shard] = jnp.zeros((DH, 1024), jnp.float32)
    for load in loads:
        load.wait()

    def place(block):
        return block // 8, pl.ds(pl.multiple_of((block % 8) * BLK, BLK), BLK)

    def pick(buf, ids):
        parts = []
        for block in ids:
            shard, cols = place(block)
            parts.append(buf[shard, :, cols])
        return jnp.concatenate(parts, axis=1)

    def spread(buf, ids, total):
        for k, block in enumerate(ids):
            shard, cols = place(block)
            buf[shard, :, cols] += total[:, k * BLK : (k + 1) * BLK]

    def one_tile(i, later):
        tile = seq * 8 + i
        tail = (count_ref[tile] - 1) % GRP
        rows = pl.ds(pl.multiple_of(i * BLK, BLK), BLK)
        q2 = q_ref[rows, :]
        do2 = do_ref[rows, :]
        q = jnp.concatenate([q2[:, :DH], q2[:, DH:]], axis=0)
        do = jnp.concatenate([do2[:, :DH], do2[:, DH:]], axis=0)

        def first_ids():
            return [tile] + [
                jnp.where(k <= tail, blocks_ref[tile, k], tile) for k in range(1, GRP)
            ]

        def later_ids(g):
            start = 1 + tail + GRP * (g - 1)
            return [blocks_ref[tile, start + k] for k in range(GRP)]

        ids0 = first_ids()
        s = dot(q, pick(kbuf, ids0))
        row = lax.broadcasted_iota(jnp.int32, (2 * BLK, BLK), 0) % BLK
        col = lax.broadcasted_iota(jnp.int32, (2 * BLK, BLK), 1)
        parts = [jnp.where(col <= row, s[:, :BLK], NEG)]
        for k in range(1, GRP):
            parts.append(jnp.where(k <= tail, s[:, k * BLK : (k + 1) * BLK], NEG))
        top = parts[0]
        for part in parts[1:]:
            top = jnp.maximum(top, part)
        scores[0] = jnp.concatenate(parts, axis=1)

        def fold_max(top, s):
            for k in range(GRP):
                top = jnp.maximum(top, s[:, k * BLK : (k + 1) * BLK])
            return top

        def pass_scores(g, top):
            s = dot(q, pick(kbuf, later_ids(g)))
            scores[g] = s
            return fold_max(top, s)
        for g in range(1, later + 1):
            top = pass_scores(g, top)
        peak = wide(jnp.max(top, axis=1, keepdims=True) * (SCALE * LOG2E))

        def forward(g, ids, carry):
            p = jnp.exp2(scores[g] * (SCALE * LOG2E) - across(peak))
            scores[g] = p
            grads[g] = dot(do, pick(vbuf, ids))
            values = jnp.concatenate(
                [pick(vbuf, ids), jnp.ones((DH, GRP * BLK), jnp.bfloat16)], axis=0
            )
            return carry + dot_nt(p.astype(jnp.bfloat16), values)

        zero = jnp.zeros((2 * BLK, BLK), jnp.float32)
        both = forward(0, ids0, jnp.zeros((2 * BLK, 2 * DH), jnp.float32))
        for g in range(1, later + 1):
            both = forward(g, later_ids(g), both)
        out, row_total = both[:, :DH], both[:, DH:]
        share = 1.0 / row_total
        attended = (out * share).astype(jnp.bfloat16)
        o_ref[rows, :] = jnp.concatenate([attended[:BLK], attended[BLK:]], axis=1)
        row_dot = jnp.sum(
            do.astype(jnp.float32) * attended.astype(jnp.float32), axis=1, keepdims=True
        )
        row_dot = across(wide(row_dot))
        share = across(share)
        q_t = jnp.transpose(q)
        do_t = jnp.transpose(do)

        def backward(g, ids, grad_q):
            w = scores[g] * share
            grad_s = (w * (grads[g] - row_dot)).astype(jnp.bfloat16)
            spread(dv, ids, dot(do_t, w.astype(jnp.bfloat16)))
            spread(dk, ids, dot(q_t, grad_s))
            return grad_q + dot_nt(grad_s, pick(kbuf, ids))

        grad_q = backward(0, ids0, zero)
        for g in range(1, later + 1):
            grad_q = backward(g, later_ids(g), grad_q)
        grad_q = (grad_q * SCALE).astype(jnp.bfloat16)
        dq_ref[rows, :] = jnp.concatenate([grad_q[:BLK], grad_q[BLK:]], axis=1)

    def any_tile(i, carry):
        full = (count_ref[seq * 8 + i] - 1) // GRP
        for v in range(NNZ // GRP):
            pl.when(full == v)(lambda v=v: one_tile(i, v))
        return carry

    lax.fori_loop(0, 8, any_tile, 0)

    stores = []
    for shard in range(8):
        for buf, low, keep, send, scale in (
            (dk, stage.at[0], k_keep, k_send, SCALE),
            (dv, stage.at[1], v_keep, v_send, None),
        ):
            value = buf[shard]
            if scale is not None:
                value = value * scale
            low[shard] = value.astype(jnp.bfloat16)
            for rows, dst in (
                (mine, keep.at[shard, 0]),
                (other_y, keep.at[shard, 1]),
                (sib, send.at[shard, 0]),
                (sib_y, send.at[shard, 1]),
            ):
                copy = pltpu.make_async_copy(low.at[shard, rows], dst, out_sem.at[len(stores)])
                copy.start()
                stores.append(copy)
    for copy in stores:
        copy.wait()


def attend(where, key_blocks, block_count, queries, grad_out, parts):
    whole = pl.BlockSpec(memory_space=pltpu.VMEM)
    scalar = pl.BlockSpec(memory_space=pltpu.SMEM)
    away = pl.BlockSpec(memory_space=pl.ANY)
    half = jax.ShapeDtypeStruct((8, 2, QUARTER, 1024), jnp.bfloat16)
    grid_q = jax.ShapeDtypeStruct(queries.shape, jnp.bfloat16)
    return pl.pallas_call(
        attend_kernel,
        in_specs=[scalar] * 3 + [whole] * 2 + [away] * 6,
        out_specs=[whole] * 2 + [away] * 4,
        out_shape=[grid_q, grid_q, half, half, half, half],
        scratch_shapes=[
            pltpu.VMEM((8, DH, 1024), jnp.bfloat16),
            pltpu.VMEM((8, DH, 1024), jnp.bfloat16),
            pltpu.VMEM((8, DH, 1024), jnp.float32),
            pltpu.VMEM((8, DH, 1024), jnp.float32),
            pltpu.VMEM((NNZ // GRP, 2 * BLK, GRP * BLK), jnp.float32),
            pltpu.VMEM((NNZ // GRP, 2 * BLK, GRP * BLK), jnp.float32),
            pltpu.VMEM((2, 8, DH, 1024), jnp.bfloat16),
            pltpu.SemaphoreType.DMA((8,)),
            pltpu.SemaphoreType.DMA((64,)),
        ],
        compiler_params=pltpu.CompilerParams(vmem_limit_bytes=48 << 20),
        name="attend",
    )(where, key_blocks, block_count, queries, grad_out, *parts)


def swap(value, bit):
    return lax.ppermute(value, "head", [(i, i ^ bit) for i in range(lax.axis_size("head"))])


def send_all(value):
    shards = lax.axis_size("seq")
    return lax.all_to_all(jnp.broadcast_to(value[None], (shards,) + value.shape), "seq", 0, 0)


def per_device(queries, key_cols, value_cols, grad_out, key_blocks, block_count):
    seq_index = lax.axis_index("seq")
    quarter = lax.axis_index("head") & 3
    upper = quarter >> 1 == 1

    v_mine = send_all(value_cols)
    k_pair = jnp.stack([key_cols, swap(key_cols, 2)])
    k_mine = send_all(k_pair)
    v_pair = swap(v_mine, 2)
    v_sib = swap(v_mine, 1)
    v_sib_pair = swap(v_pair, 1)
    k_sib = swap(k_mine, 1)

    where = jnp.stack([seq_index, quarter]).astype(jnp.int32)
    attn_out, grad_query, k_keep, k_send, v_keep, v_send = attend(
        where, key_blocks, block_count, queries, grad_out,
        (k_mine, k_sib, v_mine, v_pair, v_sib, v_sib_pair),
    )

    def add(left, right):
        return left.astype(jnp.float32) + right.astype(jnp.float32)

    v_half = add(v_keep, swap(v_send, 1)).astype(jnp.bfloat16)
    k_half = add(k_keep, swap(k_send, 1)).astype(jnp.bfloat16)
    v_quarter = add(v_half[:, 0], swap(v_half[:, 1], 2)).astype(jnp.bfloat16)
    k_got = lax.all_to_all(k_half, "seq", 0, 0)
    k_sum = jnp.sum(k_got.astype(jnp.float32), axis=0)
    v_got = lax.all_to_all(v_quarter, "seq", 0, 0)
    grad_value = jnp.sum(v_got.astype(jnp.float32), axis=0).astype(jnp.bfloat16)
    grad_key = (k_sum[0] + swap(k_sum[1], 2)).astype(jnp.bfloat16)
    return attn_out, grad_query, grad_key, grad_value


def solution(mesh):
    placed = (P("seq", "head"), P("head", "seq"), P("head", "seq"), P("seq", "head"), P(), P())
    return jax.shard_map(
        per_device,
        mesh=mesh,
        in_specs=placed,
        out_specs=(P("seq", "head"), P("seq", "head"), P("head", "seq"), P("head", "seq")),
        check_vma=False,
    )
```

```python
import math

import jax
import jax.numpy as jnp
from jax import lax
from jax.experimental import pallas as pl
from jax.experimental.pallas import tpu as pltpu
from jax.sharding import PartitionSpec as P

DH = 128
HQ_DEV = 2
BLK = 128
GRP = 4
NNZ = 24
QUARTER = 32
NEG = -1e30
SCALE = 1.0 / math.sqrt(DH)
LOG2E = 1.4426950408889634
NT = (((1,), (1,)), ((), ()))


def dot(left, right):
    return jnp.dot(left, right, preferred_element_type=jnp.float32)


def dot_nt(left, right):
    return lax.dot_general(left, right, NT, preferred_element_type=jnp.float32)


def wide(column):
    return jnp.broadcast_to(column, (column.shape[0], BLK))


def across(tile):
    return jnp.concatenate([tile] * GRP, axis=1)


def attend_kernel(
    where_ref, blocks_ref, count_ref,
    q_ref, do_ref, ka_ref, kc_ref, va_ref, vb_ref, vc_ref, vd_ref,
    o_ref, dq_ref, k_keep, k_send, v_keep, v_send,
    kbuf, vbuf, dk, dv, scores, grads, stage, in_sem, out_sem,
):
    seq = where_ref[0]
    quarter = where_ref[1]

    def rows_of(index):
        return pl.ds(pl.multiple_of(index * QUARTER, QUARTER), QUARTER)

    mine, other_y = rows_of(quarter), rows_of(quarter ^ 2)
    sib, sib_y = rows_of(quarter ^ 1), rows_of(quarter ^ 3)
    loads = []
    for src, dst in (
        (ka_ref.at[:, 0], kbuf.at[:, mine]),
        (ka_ref.at[:, 1], kbuf.at[:, other_y]),
        (kc_ref.at[:, 0], kbuf.at[:, sib]),
        (kc_ref.at[:, 1], kbuf.at[:, sib_y]),
        (va_ref, vbuf.at[:, mine]),
        (vb_ref, vbuf.at[:, other_y]),
        (vc_ref, vbuf.at[:, sib]),
        (vd_ref, vbuf.at[:, sib_y]),
    ):
        loads.append(pltpu.make_async_copy(src, dst, in_sem.at[len(loads)]))
    for load in loads:
        load.start()
    for shard in range(8):
        dk[shard] = jnp.zeros((DH, 1024), jnp.float32)
        dv[shard] = jnp.zeros((DH, 1024), jnp.float32)
    for load in loads:
        load.wait()

    def place(block):
        return block // 8, pl.ds(pl.multiple_of((block % 8) * BLK, BLK), BLK)

    def pick(buf, ids):
        parts = []
        for block in ids:
            shard, cols = place(block)
            parts.append(buf[shard, :, cols])
        return jnp.concatenate(parts, axis=1)

    def spread(buf, ids, total):
        for k, block in enumerate(ids):
            shard, cols = place(block)
            buf[shard, :, cols] += total[:, k * BLK : (k + 1) * BLK]

    def one_tile(i, later):
        tile = seq * 8 + i
        tail = (count_ref[tile] - 1) % GRP
        rows = pl.ds(pl.multiple_of(i * BLK, BLK), BLK)
        q2 = q_ref[rows, :]
        do2 = do_ref[rows, :]
        q = jnp.concatenate([q2[:, :DH], q2[:, DH:]], axis=0)
        do = jnp.concatenate([do2[:, :DH], do2[:, DH:]], axis=0)

        def first_ids():
            return [tile] + [
                jnp.where(k <= tail, blocks_ref[tile, k], tile) for k in range(1, GRP)
            ]

        def later_ids(g):
            start = 1 + tail + GRP * (g - 1)
            return [blocks_ref[tile, start + k] for k in range(GRP)]

        ids0 = first_ids()
        s = dot(q, pick(kbuf, ids0))
        row = lax.broadcasted_iota(jnp.int32, (2 * BLK, BLK), 0) % BLK
        col = lax.broadcasted_iota(jnp.int32, (2 * BLK, BLK), 1)
        parts = [jnp.where(col <= row, s[:, :BLK], NEG)]
        for k in range(1, GRP):
            parts.append(jnp.where(k <= tail, s[:, k * BLK : (k + 1) * BLK], NEG))
        top = parts[0]
        for part in parts[1:]:
            top = jnp.maximum(top, part)
        scores[0] = jnp.concatenate(parts, axis=1)

        def fold_max(top, s):
            for k in range(GRP):
                top = jnp.maximum(top, s[:, k * BLK : (k + 1) * BLK])
            return top

        def pass_scores(g, top):
            s = dot(q, pick(kbuf, later_ids(g)))
            scores[g] = s
            return fold_max(top, s)
        for g in range(1, later + 1):
            top = pass_scores(g, top)
        peak = wide(jnp.max(top, axis=1, keepdims=True) * (SCALE * LOG2E))

        def forward(g, ids, carry):
            p = jnp.exp2(scores[g] * (SCALE * LOG2E) - across(peak))
            scores[g] = p
            grads[g] = dot(do, pick(vbuf, ids))
            values = jnp.concatenate(
                [pick(vbuf, ids), jnp.ones((DH, GRP * BLK), jnp.bfloat16)], axis=0
            )
            return carry + dot_nt(p.astype(jnp.bfloat16), values)

        zero = jnp.zeros((2 * BLK, BLK), jnp.float32)
        both = forward(0, ids0, jnp.zeros((2 * BLK, 2 * DH), jnp.float32))
        for g in range(1, later + 1):
            both = forward(g, later_ids(g), both)
        out, row_total = both[:, :DH], both[:, DH:]
        share = 1.0 / row_total
        attended = (out * share).astype(jnp.bfloat16)
        o_ref[rows, :] = jnp.concatenate([attended[:BLK], attended[BLK:]], axis=1)
        row_dot = jnp.sum(
            do.astype(jnp.float32) * attended.astype(jnp.float32), axis=1, keepdims=True
        )
        row_dot = across(wide(row_dot))
        share = across(share)
        q_t = jnp.transpose(q)
        do_t = jnp.transpose(do)

        def backward(g, ids, grad_q):
            w = scores[g] * share
            grad_s = (w * (grads[g] - row_dot)).astype(jnp.bfloat16)
            spread(dv, ids, dot(do_t, w.astype(jnp.bfloat16)))
            spread(dk, ids, dot(q_t, grad_s))
            return grad_q + dot_nt(grad_s, pick(kbuf, ids))

        grad_q = backward(0, ids0, zero)
        for g in range(1, later + 1):
            grad_q = backward(g, later_ids(g), grad_q)
        grad_q = (grad_q * SCALE).astype(jnp.bfloat16)
        dq_ref[rows, :] = jnp.concatenate([grad_q[:BLK], grad_q[BLK:]], axis=1)

    def any_tile(i, carry):
        full = (count_ref[seq * 8 + i] - 1) // GRP
        for v in range(NNZ // GRP):
            pl.when(full == v)(lambda v=v: one_tile(i, v))
        return carry

    lax.fori_loop(0, 8, any_tile, 0)

    stores = []
    for shard in range(8):
        for buf, low, keep, send, scale in (
            (dk, stage.at[0], k_keep, k_send, SCALE),
            (dv, stage.at[1], v_keep, v_send, None),
        ):
            value = buf[shard]
            if scale is not None:
                value = value * scale
            low[shard] = value.astype(jnp.bfloat16)
            for rows, dst in (
                (mine, keep.at[shard, 0]),
                (other_y, keep.at[shard, 1]),
                (sib, send.at[shard, 0]),
                (sib_y, send.at[shard, 1]),
            ):
                copy = pltpu.make_async_copy(low.at[shard, rows], dst, out_sem.at[len(stores)])
                copy.start()
                stores.append(copy)
    for copy in stores:
        copy.wait()


def attend(where, key_blocks, block_count, queries, grad_out, parts):
    whole = pl.BlockSpec(memory_space=pltpu.VMEM)
    scalar = pl.BlockSpec(memory_space=pltpu.SMEM)
    away = pl.BlockSpec(memory_space=pl.ANY)
    half = jax.ShapeDtypeStruct((8, 2, QUARTER, 1024), jnp.bfloat16)
    grid_q = jax.ShapeDtypeStruct(queries.shape, jnp.bfloat16)
    return pl.pallas_call(
        attend_kernel,
        in_specs=[scalar] * 3 + [whole] * 2 + [away] * 6,
        out_specs=[whole] * 2 + [away] * 4,
        out_shape=[grid_q, grid_q, half, half, half, half],
        scratch_shapes=[
            pltpu.VMEM((8, DH, 1024), jnp.bfloat16),
            pltpu.VMEM((8, DH, 1024), jnp.bfloat16),
            pltpu.VMEM((8, DH, 1024), jnp.float32),
            pltpu.VMEM((8, DH, 1024), jnp.float32),
            pltpu.VMEM((NNZ // GRP, 2 * BLK, GRP * BLK), jnp.float32),
            pltpu.VMEM((NNZ // GRP, 2 * BLK, GRP * BLK), jnp.float32),
            pltpu.VMEM((2, 8, DH, 1024), jnp.bfloat16),
            pltpu.SemaphoreType.DMA((8,)),
            pltpu.SemaphoreType.DMA((64,)),
        ],
        compiler_params=pltpu.CompilerParams(vmem_limit_bytes=48 << 20),
        name="attend",
    )(where, key_blocks, block_count, queries, grad_out, *parts)


def swap(value, bit):
    return lax.ppermute(value, "head", [(i, i ^ bit) for i in range(lax.axis_size("head"))])


def send_all(value):
    shards = lax.axis_size("seq")
    return lax.all_to_all(jnp.broadcast_to(value[None], (shards,) + value.shape), "seq", 0, 0)


def per_device(queries, key_cols, value_cols, grad_out, key_blocks, block_count):
    seq_index = lax.axis_index("seq")
    quarter = lax.axis_index("head") & 3
    upper = quarter >> 1 == 1

    v_mine = send_all(value_cols)
    k_pair = jnp.stack([key_cols, swap(key_cols, 2)])
    k_mine = send_all(k_pair)
    v_pair = swap(v_mine, 2)
    v_sib = swap(v_mine, 1)
    v_sib_pair = swap(v_pair, 1)
    k_sib = swap(k_mine, 1)

    where = jnp.stack([seq_index, quarter]).astype(jnp.int32)
    attn_out, grad_query, k_keep, k_send, v_keep, v_send = attend(
        where, key_blocks, block_count, queries, grad_out,
        (k_mine, k_sib, v_mine, v_pair, v_sib, v_sib_pair),
    )

    def add(left, right):
        return left.astype(jnp.float32) + right.astype(jnp.float32)

    v_half = add(v_keep, swap(v_send, 1)).astype(jnp.bfloat16)
    k_half = add(k_keep, swap(k_send, 1)).astype(jnp.bfloat16)
    v_quarter = add(v_half[:, 0], swap(v_half[:, 1], 2)).astype(jnp.bfloat16)
    k_got = lax.all_to_all(k_half, "seq", 0, 0)
    k_sum = jnp.sum(k_got.astype(jnp.float32), axis=0)
    v_got = lax.all_to_all(v_quarter, "seq", 0, 0)
    grad_key = (k_sum[0] + swap(k_sum[1], 2)).astype(jnp.bfloat16)
    v_got, grad_key = lax.optimization_barrier((v_got, grad_key))
    grad_value = jnp.sum(v_got.astype(jnp.float32), axis=0).astype(jnp.bfloat16)
    return attn_out, grad_query, grad_key, grad_value


def solution(mesh):
    placed = (P("seq", "head"), P("head", "seq"), P("head", "seq"), P("seq", "head"), P(), P())
    return jax.shard_map(
        per_device,
        mesh=mesh,
        in_specs=placed,
        out_specs=(P("seq", "head"), P("seq", "head"), P("head", "seq"), P("head", "seq")),
        check_vma=False,
    )
```

```python
import math

import jax
import jax.numpy as jnp
from jax import lax
from jax.experimental import pallas as pl
from jax.experimental.pallas import tpu as pltpu
from jax.sharding import PartitionSpec as P

DH = 128
HQ_DEV = 2
BLK = 128
GRP = 4
NNZ = 24
QUARTER = 32
NEG = -1e30
SCALE = 1.0 / math.sqrt(DH)
LOG2E = 1.4426950408889634
NT = (((1,), (1,)), ((), ()))


def dot(left, right):
    return jnp.dot(left, right, preferred_element_type=jnp.float32)


def dot_nt(left, right):
    return lax.dot_general(left, right, NT, preferred_element_type=jnp.float32)


def wide(column):
    return jnp.broadcast_to(column, (column.shape[0], BLK))


def across(tile):
    return jnp.concatenate([tile] * GRP, axis=1)


def attend_kernel(
    where_ref, blocks_ref, count_ref,
    q_ref, do_ref, ka_ref, kc_ref, va_ref, vb_ref, vc_ref, vd_ref,
    o_ref, dq_ref, k_keep, k_send, v_keep, v_send,
    kbuf, vbuf, dk, dv, scores, grads, stage, in_sem, out_sem,
):
    seq = where_ref[0]
    quarter = where_ref[1]

    def rows_of(index):
        return pl.ds(pl.multiple_of(index * QUARTER, QUARTER), QUARTER)

    mine, other_y = rows_of(quarter), rows_of(quarter ^ 2)
    sib, sib_y = rows_of(quarter ^ 1), rows_of(quarter ^ 3)
    loads = []
    for src, dst in (
        (ka_ref.at[:, 0], kbuf.at[:, mine]),
        (ka_ref.at[:, 1], kbuf.at[:, other_y]),
        (kc_ref.at[:, 0], kbuf.at[:, sib]),
        (kc_ref.at[:, 1], kbuf.at[:, sib_y]),
        (va_ref, vbuf.at[:, mine]),
        (vb_ref, vbuf.at[:, other_y]),
        (vc_ref, vbuf.at[:, sib]),
        (vd_ref, vbuf.at[:, sib_y]),
    ):
        loads.append(pltpu.make_async_copy(src, dst, in_sem.at[len(loads)]))
    for load in loads:
        load.start()
    for shard in range(8):
        dk[shard] = jnp.zeros((DH, 1024), jnp.float32)
        dv[shard] = jnp.zeros((DH, 1024), jnp.float32)
    for load in loads:
        load.wait()

    def place(block):
        return block // 8, pl.ds(pl.multiple_of((block % 8) * BLK, BLK), BLK)

    def pick(buf, ids):
        parts = []
        for block in ids:
            shard, cols = place(block)
            parts.append(buf[shard, :, cols])
        return jnp.concatenate(parts, axis=1)

    def spread(buf, ids, total):
        for k, block in enumerate(ids):
            shard, cols = place(block)
            buf[shard, :, cols] += total[:, k * BLK : (k + 1) * BLK]

    def one_tile(i, later):
        tile = seq * 8 + i
        tail = (count_ref[tile] - 1) % GRP
        rows = pl.ds(pl.multiple_of(i * BLK, BLK), BLK)
        q2 = q_ref[rows, :]
        do2 = do_ref[rows, :]
        q = jnp.concatenate([q2[:, :DH], q2[:, DH:]], axis=0)
        do = jnp.concatenate([do2[:, :DH], do2[:, DH:]], axis=0)

        def first_ids():
            return [tile] + [
                jnp.where(k <= tail, blocks_ref[tile, k], tile) for k in range(1, GRP)
            ]

        def later_ids(g):
            start = 1 + tail + GRP * (g - 1)
            return [blocks_ref[tile, start + k] for k in range(GRP)]

        ids0 = first_ids()
        s = dot(q, pick(kbuf, ids0))
        row = lax.broadcasted_iota(jnp.int32, (2 * BLK, BLK), 0) % BLK
        col = lax.broadcasted_iota(jnp.int32, (2 * BLK, BLK), 1)
        parts = [jnp.where(col <= row, s[:, :BLK], NEG)]
        for k in range(1, GRP):
            parts.append(jnp.where(k <= tail, s[:, k * BLK : (k + 1) * BLK], NEG))
        top = parts[0]
        for part in parts[1:]:
            top = jnp.maximum(top, part)
        scores[0] = jnp.concatenate(parts, axis=1)

        def fold_max(top, s):
            for k in range(GRP):
                top = jnp.maximum(top, s[:, k * BLK : (k + 1) * BLK])
            return top

        def pass_scores(g, top):
            s = dot(q, pick(kbuf, later_ids(g)))
            scores[g] = s
            return fold_max(top, s)
        for g in range(1, later + 1):
            top = pass_scores(g, top)
        peak = wide(jnp.max(top, axis=1, keepdims=True) * (SCALE * LOG2E))

        def forward(g, ids, carry):
            p = jnp.exp2(scores[g] * (SCALE * LOG2E) - across(peak))
            scores[g] = p
            grads[g] = dot(do, pick(vbuf, ids))
            values = jnp.concatenate(
                [pick(vbuf, ids), jnp.ones((DH, GRP * BLK), jnp.bfloat16)], axis=0
            )
            return carry + dot_nt(p.astype(jnp.bfloat16), values)

        zero = jnp.zeros((2 * BLK, BLK), jnp.float32)
        both = forward(0, ids0, jnp.zeros((2 * BLK, 2 * DH), jnp.float32))
        for g in range(1, later + 1):
            both = forward(g, later_ids(g), both)
        out, row_total = both[:, :DH], both[:, DH:]
        share = 1.0 / row_total
        attended = (out * share).astype(jnp.bfloat16)
        o_ref[rows, :] = jnp.concatenate([attended[:BLK], attended[BLK:]], axis=1)
        row_dot = jnp.sum(
            do.astype(jnp.float32) * attended.astype(jnp.float32), axis=1, keepdims=True
        )
        row_dot = across(wide(row_dot))
        share = across(share)
        q_t = jnp.transpose(q)
        do_t = jnp.transpose(do)

        def backward(g, ids, grad_q):
            w = scores[g] * share
            grad_s = (w * (grads[g] - row_dot)).astype(jnp.bfloat16)
            spread(dv, ids, dot(do_t, w.astype(jnp.bfloat16)))
            spread(dk, ids, dot(q_t, grad_s))
            return grad_q + dot_nt(grad_s, pick(kbuf, ids))

        grad_q = backward(0, ids0, zero)
        for g in range(1, later + 1):
            grad_q = backward(g, later_ids(g), grad_q)
        grad_q = (grad_q * SCALE).astype(jnp.bfloat16)
        dq_ref[rows, :] = jnp.concatenate([grad_q[:BLK], grad_q[BLK:]], axis=1)

    def any_tile(i, carry):
        full = (count_ref[seq * 8 + i] - 1) // GRP
        for v in range(NNZ // GRP):
            pl.when(full == v)(lambda v=v: one_tile(i, v))
        return carry

    lax.fori_loop(0, 8, any_tile, 0)

    stores = []
    for shard in range(8):
        for buf, low, keep, send, scale in (
            (dk, stage.at[0], k_keep, k_send, SCALE),
            (dv, stage.at[1], v_keep, v_send, None),
        ):
            value = buf[shard]
            if scale is not None:
                value = value * scale
            low[shard] = value.astype(jnp.bfloat16)
            for rows, dst in (
                (mine, keep.at[shard, 0]),
                (other_y, keep.at[shard, 1]),
                (sib, send.at[shard, 0]),
                (sib_y, send.at[shard, 1]),
            ):
                copy = pltpu.make_async_copy(low.at[shard, rows], dst, out_sem.at[len(stores)])
                copy.start()
                stores.append(copy)
    for copy in stores:
        copy.wait()


def attend(where, key_blocks, block_count, queries, grad_out, parts):
    whole = pl.BlockSpec(memory_space=pltpu.VMEM)
    scalar = pl.BlockSpec(memory_space=pltpu.SMEM)
    away = pl.BlockSpec(memory_space=pl.ANY)
    half = jax.ShapeDtypeStruct((8, 2, QUARTER, 1024), jnp.bfloat16)
    grid_q = jax.ShapeDtypeStruct(queries.shape, jnp.bfloat16)
    return pl.pallas_call(
        attend_kernel,
        in_specs=[scalar] * 3 + [whole] * 2 + [away] * 6,
        out_specs=[whole] * 2 + [away] * 4,
        out_shape=[grid_q, grid_q, half, half, half, half],
        scratch_shapes=[
            pltpu.VMEM((8, DH, 1024), jnp.bfloat16),
            pltpu.VMEM((8, DH, 1024), jnp.bfloat16),
            pltpu.VMEM((8, DH, 1024), jnp.float32),
            pltpu.VMEM((8, DH, 1024), jnp.float32),
            pltpu.VMEM((NNZ // GRP, 2 * BLK, GRP * BLK), jnp.float32),
            pltpu.VMEM((NNZ // GRP, 2 * BLK, GRP * BLK), jnp.float32),
            pltpu.VMEM((2, 8, DH, 1024), jnp.bfloat16),
            pltpu.SemaphoreType.DMA((8,)),
            pltpu.SemaphoreType.DMA((64,)),
        ],
        compiler_params=pltpu.CompilerParams(vmem_limit_bytes=48 << 20),
        name="attend",
    )(where, key_blocks, block_count, queries, grad_out, *parts)


def swap(value, bit):
    return lax.ppermute(value, "head", [(i, i ^ bit) for i in range(lax.axis_size("head"))])


def send_all(value):
    shards = lax.axis_size("seq")
    return lax.all_to_all(jnp.broadcast_to(value[None], (shards,) + value.shape), "seq", 0, 0)


def per_device(queries, key_cols, value_cols, grad_out, key_blocks, block_count):
    seq_index = lax.axis_index("seq")
    quarter = lax.axis_index("head") & 3
    upper = quarter >> 1 == 1

    v_mine = send_all(value_cols)
    k_pair = jnp.stack([key_cols, swap(key_cols, 2)])
    k_mine = send_all(k_pair)
    v_pair = swap(v_mine, 2)
    v_sib = swap(v_mine, 1)
    v_sib_pair = swap(v_pair, 1)
    k_sib = swap(k_mine, 1)

    where = jnp.stack([seq_index, quarter]).astype(jnp.int32)
    attn_out, grad_query, k_keep, k_send, v_keep, v_send = attend(
        where, key_blocks, block_count, queries, grad_out,
        (k_mine, k_sib, v_mine, v_pair, v_sib, v_sib_pair),
    )

    def add(left, right):
        return left.astype(jnp.float32) + right.astype(jnp.float32)

    v_got_half = swap(v_send, 1)
    v_away = add(v_keep[:, 1], v_got_half[:, 1]).astype(jnp.bfloat16)
    k_half = add(k_keep, swap(k_send, 1)).astype(jnp.bfloat16)
    v_mine_sum = add(v_keep[:, 0], v_got_half[:, 0])
    v_quarter = add(v_mine_sum, swap(v_away, 2)).astype(jnp.bfloat16)
    k_got = lax.all_to_all(k_half, "seq", 0, 0)
    k_sum = jnp.sum(k_got.astype(jnp.float32), axis=0)
    v_got = lax.all_to_all(v_quarter, "seq", 0, 0)
    grad_key = (k_sum[0] + swap(k_sum[1], 2)).astype(jnp.bfloat16)
    v_got, grad_key = lax.optimization_barrier((v_got, grad_key))
    grad_value = jnp.sum(v_got.astype(jnp.float32), axis=0).astype(jnp.bfloat16)
    return attn_out, grad_query, grad_key, grad_value


def solution(mesh):
    placed = (P("seq", "head"), P("head", "seq"), P("head", "seq"), P("seq", "head"), P(), P())
    return jax.shard_map(
        per_device,
        mesh=mesh,
        in_specs=placed,
        out_specs=(P("seq", "head"), P("seq", "head"), P("head", "seq"), P("head", "seq")),
        check_vma=False,
    )
```
